1024 devices in a mesh: ctx: 16 (over z), head: 64 (over x, y, core).
Axes of the slice: x: 4, y: 8, z: 16, core: 2. Of those that a mesh axis runs over, the one named last changes fastest.
Arguments:
- out_grad: bfloat16 [6144, 8192], P('ctx', 'head'), may hold values from -0.1796875 to 0.1796875
- conv_input: bfloat16 [6144, 8192], P('ctx', 'head'), may hold values from -0.119628906 to 0.119628906
- residues: float32 [16, 8192], P(None, 'head'), may hold values from -1.5 to 1.5
- decay_rate: float32 [16, 8192], P(None, 'head'), may hold values from 1e-05 to 0.033
- segments: int32 [6144], replicated, may hold values from 0 to 3, never falling along the last dimension, each value on 1 to 3072 neighbouring positions
- w_in: bfloat16 [8192, 8192], P('head'), may hold values from -0.0625 to 0.0625
Outputs:
- d_input: bfloat16 [6144, 8192], P('ctx', 'head')
- filter_grad: float32 [16, 8192], P(None, 'head')
The draws below stay inside these ranges and needn't reach their ends.
Inputs may be any that keep to these rules, and one draw needn't show every extreme that they name: `segments`: document numbers never fall along the tokens; every document has 1 to 3072 tokens and one has exactly 3072.
All inputs are finite; a program needn't handle non-finite values.
Results may differ from the reference program's by a relative error of at most 0.0049.
Values may be sent and summed in bfloat16 or wider, within the bound.
No kernel may reach another device: no remote copies, remote signals or barrier semaphores. Data moves between devices by JAX's collectives and lax.ppermute only.
A program may use at most 32 MiB of HBM per device.

```python
import math
import jax
import jax.numpy as jnp
import numpy as np
from jax import lax

D = 8192
MODES = 16
DOCS = 4
TOKENS = 6144


def level_of(own_key, shape, shards, least, top_value):
    def one(axis_at, parts):
        draws = jax.random.uniform(jax.random.fold_in(jax.random.fold_in(own_key, 6), axis_at), (parts,), jnp.float32, least / len(shards), top_value / len(shards))
        return jnp.repeat(jnp.exp(draws), shape[axis_at] // parts).reshape((-1,) + (1,) * (len(shape) - axis_at - 1))

    level = one(*shards[0])
    for cut in shards[1:]:
        level = level * one(*cut)
    return level


def length_profile(amount, total, most, slope):
    loads = [(1 << 20) // math.isqrt(rank ** slope) + 1 for rank in range(2, amount + 1)]
    spare, given = total - most - (amount - 1), [1] * (amount - 1)
    while spare > 0:
        free = [i for i in range(amount - 1) if given[i] < most]
        whole, remaining = sum([loads[i] for i in free]), spare
        for i in free:
            extra = min(most - given[i], max(1, remaining * loads[i] // whole), spare)
            given[i] = given[i] + extra
            spare = spare - extra
    return np.array([most] + given)


def uneven(key, count, total, most, skew):
    if count == 2:
        one = jax.random.randint(key, (), max(1, total - most), min(most, total - 1) + 1)
        return jnp.stack([one, total - one])
    lengths = jnp.asarray(length_profile(count, total, most, skew), jnp.int32)
    twos = (count - 1) // 2
    source_of, taker = lengths[1:1 + 2 * twos:2], lengths[2:2 + 2 * twos:2]
    room = jnp.minimum(source_of - 1, most - taker)
    moved = jax.random.randint(jax.random.fold_in(key, 1), (twos,), 0, 1 << 20) % (room + 1)
    lengths = lengths.at[1:1 + 2 * twos:2].set(source_of - moved).at[2:2 + 2 * twos:2].set(taker + moved)
    return lengths[jax.random.permutation(jax.random.fold_in(key, 2), count)]


def gaussian(rng, dims, scale, reach, shards=(), kind=jnp.bfloat16):
    array = scale * jax.random.normal(rng, dims, jnp.float32)
    if shards:
        array = array * level_of(rng, dims, shards, -0.22, 0.18)
    return jnp.clip(array, -reach, reach).astype(kind)


def setup_inputs(seed: int = 0) -> dict:
    seeds = jax.random.split(jax.random.key(seed), 7)
    out_grad = gaussian(seeds[0], (TOKENS, D), 0.03, 0.1796875, ((0, 16), (1, 64)))
    conv_input = gaussian(seeds[1], (TOKENS, D), 0.02, 0.119628906, ((0, 16), (1, 64)))
    residues = gaussian(seeds[2], (MODES, D), MODES ** -0.5, 1.5, ((1, 64),), jnp.float32)
    decay_rate = jnp.clip(jnp.exp(math.log(0.033) - 8.101678 * jax.random.uniform(seeds[3], (MODES, D), jnp.float32) ** level_of(seeds[3], (MODES, D), ((1, 64),), -0.2, 0.2)), 9.999999747378752e-06, 0.033)
    segments = jnp.searchsorted(jnp.cumsum(uneven(seeds[4], DOCS, TOKENS, TOKENS // 2, 0)), jnp.arange(TOKENS), side="right").astype(jnp.int32)
    w_in = gaussian(seeds[5], (D, D), D ** -0.5, 0.0625, ((0, 64),))
    return dict(out_grad=out_grad, conv_input=conv_input, residues=residues, decay_rate=decay_rate, segments=segments, w_in=w_in)


def reference(out_grad, conv_input, residues, decay_rate, segments, w_in):
    decay_factor = jnp.exp(-decay_rate)
    following = jnp.concatenate([segments[1:], jnp.full((1,), -1, jnp.int32)])
    link_flags = (segments == following).astype(jnp.float32)
    grad_rows = out_grad.astype(jnp.float32)
    input_rows = conv_input.astype(jnp.float32)

    def scan_step(state, scan_items):
        adjoint, filter_acc = state
        grad_row, input_row, link_flag = scan_items
        adjoint = grad_row[None, :] + link_flag * decay_factor * adjoint
        filter_acc = filter_acc + input_row[None, :] * adjoint
        conv_row = jnp.sum(residues * adjoint, axis=0)
        return (adjoint, filter_acc), conv_row

    zero_state = jnp.zeros(decay_factor.shape, jnp.float32)
    final_state, conv_grad = lax.scan(scan_step, (zero_state, zero_state), (grad_rows, input_rows, link_flags), reverse=True)
    filter_grad = final_state[1]
    conv_bf = conv_grad.astype(jnp.bfloat16)
    d_input = jnp.dot(conv_bf, w_in.T, preferred_element_type=jnp.float32).astype(jnp.bfloat16)
    return d_input, filter_grad
```

```python
import jax
import jax.numpy as jnp
from jax import lax
from jax.experimental import pallas as pl
from jax.experimental.pallas import tpu as pltpu
from jax.sharding import Mesh, PartitionSpec as P


LANES = 128
SUB = 8
F32 = jnp.float32
BF16 = jnp.bfloat16

VM = pl.BlockSpec(memory_space=pltpu.VMEM)
SM = pl.BlockSpec(memory_space=pltpu.SMEM)
HB = pl.BlockSpec(memory_space=pl.ANY)


def scan_kernel(
    shards, fan_x, fan_y,
    seg_ref, g_ref, x_ref, res_ref, rate_ref, w_ref,
    heads_ref, base_ref, parts_ref, keep_ref, give_ref, first_ref,
    gf, xf, prod, head_v, w_v, w_sem, ws_sem, head_sem,
):
    rows = g_ref.shape[0]
    base = lax.axis_index("z") * rows
    w_in = pltpu.make_async_copy(w_ref, w_v, w_sem)
    w_in.start()
    gf[...] = g_ref[...].astype(F32)
    xf[...] = x_ref[...].astype(F32)
    decay = jnp.exp(-rate_ref[...])
    d0, d1 = decay[:SUB], decay[SUB:]
    r0, r1 = res_ref[:SUB], res_ref[SUB:]
    zero = jnp.zeros((SUB, LANES), F32)
    one = jnp.ones((SUB, LANES), F32)

    def block(i, carry):
        a0, a1, f0, f1, g0, g1, c0, c1, nxt, run, first = carry
        top = rows - 16 * (i + 1)
        for k in range(15, -1, -1):
            t = top + k
            seg = seg_ref[base + t]
            same = seg == nxt
            nxt = seg
            run = jnp.logical_and(run, same)
            first = jnp.where(run, t, first)
            link = jnp.where(same, 1.0, 0.0).astype(F32)
            e0, e1 = d0 * link, d1 * link
            g = row(gf, t)
            x = row(xf, t)
            a0 = g + e0 * a0
            a1 = g + e1 * a1
            g0 = e0 * g0
            g1 = e1 * g1
            f0 = f0 + x * a0
            f1 = f1 + x * a1
            c0 = c0 + x * g0
            c1 = c1 + x * g1
            prod[pl.ds(pl.multiple_of(t * SUB, SUB), SUB), :] = r0 * a0 + r1 * a1
        return a0, a1, f0, f1, g0, g1, c0, c1, nxt, run, first

    last = seg_ref[base + rows - 1]
    init = (zero, zero, zero, zero, one, one, zero, zero, last, jnp.bool_(True), jnp.int32(rows - 1))
    a0, a1, f0, f1, _, _, c0, c1, _, _, first = lax.fori_loop(0, rows // 16, block, init)
    head_v[:SUB] = a0
    head_v[SUB:] = a1
    heads = [
        pltpu.make_async_copy(head_v, heads_ref.at[i], head_sem.at[i]) for i in range(shards)
    ]
    for c in heads:
        c.start()
    w_in.wait()
    width = w_v.shape[1] // (2 * fan_x * fan_y)
    mine = lax.axis_index("c")
    here = lax.axis_index("x")
    splits = []
    for k in range(fan_x):
        to = lax.rem(here + k, fan_x)
        for y in range(fan_y):
            for other, dst in ((0, keep_ref), (1, give_ref)):
                core = 1 - mine if other else mine
                at = pl.multiple_of(((to * fan_y + y) * 2 + core) * width, width)
                splits.append(
                    pltpu.make_async_copy(
                        w_v.at[:, pl.ds(at, width)],
                        dst.at[k, :, pl.ds(y * width, width)],
                        ws_sem.at[(k * fan_y + y) * 2 + other],
                    )
                )
    for c in splits:
        c.start()
    parts_ref[:SUB] = f0
    parts_ref[SUB : 2 * SUB] = f1
    parts_ref[2 * SUB : 3 * SUB] = c0
    parts_ref[3 * SUB :] = c1

    def fold(i, _):
        at = pl.multiple_of(i * 16, 16)
        total = prod[pl.ds(at * SUB, 16, stride=SUB), :]
        for k in range(1, SUB):
            total = total + prod[pl.ds(at * SUB + k, 16, stride=SUB), :]
        base_ref[pl.ds(at, 16), :] = total
        return 0

    lax.fori_loop(0, rows // 16, fold, 0)
    first_ref[...] = jnp.full((SUB, LANES), first, jnp.int32)
    for c in heads + splits:
        c.wait()


def marks_kernel(shards, rows, seg_ref, marks_ref):
    for i in range(shards):
        begin = seg_ref[i * rows]
        end = seg_ref[i * rows + rows - 1]
        whole = jnp.where(begin == end, 1.0, 0.0).astype(F32)
        marks_ref[pl.ds(i, 1), :] = jnp.full((1, LANES), whole, F32)
        if i + 1 < shards:
            on = jnp.where(end == seg_ref[(i + 1) * rows], 1.0, 0.0).astype(F32)
        else:
            on = jnp.float32(0.0)
        marks_ref[pl.ds(shards + i, 1), :] = jnp.full((1, LANES), on, F32)


def row(ref, at):
    return ref[pl.ds(at, SUB, stride=0), :]


def chain(heads_ref, marks_ref, rate, rows, visit):
    shards = heads_ref.shape[0]
    leap = jnp.exp(-float(rows) * rate)
    l0, l1 = leap[:SUB], leap[SUB:]
    in0 = in1 = jnp.zeros((SUB, LANES), F32)
    for i in range(shards - 1, -1, -1):
        visit(i, in0, in1)
        if i:
            whole = row(marks_ref, i)
            on = row(marks_ref, shards + i - 1)
            in0 = on * (heads_ref[i, :SUB] + whole * l0 * in0)
            in1 = on * (heads_ref[i, SUB:] + whole * l1 * in1)


def finish_kernel(
    heads_ref, marks_ref, res_ref, rate_ref, base_ref, parts_ref, first_ref,
    pay_ref, taps_ref, amp_v, pay_v, pay_sem,
):
    rows = base_ref.shape[0]
    modes = res_ref.shape[0]
    me = lax.axis_index("z")
    own = [jnp.zeros((SUB, LANES), F32)] * 2

    def visit(i, in0, in1):
        own[0] = jnp.where(me == i, in0, own[0])
        own[1] = jnp.where(me == i, in1, own[1])

    chain(heads_ref, marks_ref, rate_ref[...], rows, visit)
    taps_ref[:SUB] = parts_ref[:SUB] + parts_ref[2 * SUB : 3 * SUB] * own[0]
    taps_ref[SUB:] = parts_ref[SUB : 2 * SUB] + parts_ref[3 * SUB :] * own[1]
    amp_v[:SUB] = own[0] * res_ref[:SUB]
    amp_v[SUB:] = own[1] * res_ref[SUB:]
    first = first_ref[...]
    place = lax.broadcasted_iota(jnp.int32, (SUB, LANES), 0)
    back = (SUB - place).astype(F32)
    steps, terms = [], []
    for m in range(modes):
        rate = row(rate_ref, m)
        steps.append(jnp.exp(rate * -float(SUB)))
        terms.append(row(amp_v, m) * jnp.exp(rate * -back))

    def tokens(i, terms):
        terms = list(terms)
        at = pl.multiple_of(rows - 16 * (i + 1), 16)
        halves = []
        for h in (1, 0):
            tree = list(terms)
            while len(tree) > 1:
                tree = [tree[k] + tree[k + 1] for k in range(0, len(tree), 2)]
            halves.append(jnp.where(place + (at + SUB * h) >= first, tree[0], 0.0))
            terms = [a * b for a, b in zip(terms, steps)]
        carry = jnp.concatenate([halves[1], halves[0]], axis=0)
        pay_v[pl.ds(at, 16), :] = (base_ref[pl.ds(at, 16), :] + carry).astype(BF16)
        return tuple(terms)

    lax.fori_loop(0, rows // 16, tokens, tuple(terms))
    pays = [
        pltpu.make_async_copy(pay_v, pay_ref.at[i], pay_sem.at[i]) for i in range(pay_ref.shape[0])
    ]
    for c in pays:
        c.start()
    for c in pays:
        c.wait()


def product_kernel(pay_ref, *refs):
    w_refs, out_ref, conv = refs[:-2], refs[-2], refs[-1]
    fan_x = len(w_refs)
    mine = lax.axis_index("c")
    here = lax.axis_index("x")
    for y in range(pay_ref.shape[0]):
        conv[:, y * LANES : (y + 1) * LANES] = pay_ref[y]
    for k in range(fan_x):
        pair = lax.dot_general(
            conv[...], w_refs[k][...], (((1,), (1,)), ((), ())), preferred_element_type=F32
        )
        to = 2 * lax.rem(here + fan_x - k, fan_x)
        out_ref[to + mine] = pair[:, :LANES].astype(BF16)
        out_ref[to + 1 - mine] = pair[:, LANES:].astype(BF16)


def sum_kernel(parts_ref, out_ref):
    total = parts_ref[0].astype(F32)
    for i in range(1, parts_ref.shape[0]):
        total = total + parts_ref[i].astype(F32)
    out_ref[...] = total.astype(BF16)


def cost(flops, nbytes):
    return pl.CostEstimate(flops=flops, bytes_accessed=nbytes, transcendentals=0)


def device(out_grad, conv_input, residues, decay_rate, segments, w_in):
    shards, fan_x, fan_y = (lax.axis_size(n) for n in ("z", "x", "y"))
    rows, chans = out_grad.shape
    modes = residues.shape[0]
    feats, depth = w_in.shape[0], w_in.shape[1] // (2 * fan_x)
    sem = pltpu.SemaphoreType.DMA
    whole = pltpu.CompilerParams(vmem_limit_bytes=67_000_000)
    small = pltpu.CompilerParams(vmem_limit_bytes=16 * 2**20)
    heads, base, parts, keep, give, first = pl.pallas_call(
        lambda *refs: scan_kernel(shards, fan_x, fan_y, *refs),
        name="scan",
        out_shape=(
            jax.ShapeDtypeStruct((shards, modes, chans), F32),
            jax.ShapeDtypeStruct((rows, chans), F32),
            jax.ShapeDtypeStruct((2 * modes, chans), F32),
            jax.ShapeDtypeStruct((fan_x, feats, depth), BF16),
            jax.ShapeDtypeStruct((fan_x, feats, depth), BF16),
            jax.ShapeDtypeStruct((SUB, chans), jnp.int32),
        ),
        in_specs=[SM, VM, VM, VM, VM, HB],
        out_specs=(HB, VM, VM, HB, HB, VM),
        scratch_shapes=[
            pltpu.VMEM((rows, chans), F32), pltpu.VMEM((rows, chans), F32),
            pltpu.VMEM((rows * SUB, chans), F32), pltpu.VMEM((modes, chans), F32),
            pltpu.VMEM(w_in.shape, BF16),
            sem(()), sem((2 * fan_x * fan_y,)), sem((shards,)),
        ],
        compiler_params=whole,
        cost_estimate=cost(10_000_000, 8_000_000),
    )(segments, out_grad, conv_input, residues, decay_rate, w_in)

    heads_in = lax.all_to_all(heads, "z", 0, 0)
    got = lax.ppermute(give, "c", [(0, 1), (1, 0)])
    weights = []
    for k in range(fan_x):
        pair = jnp.concatenate([keep[k], got[k]], axis=0)
        if k:
            pair = lax.ppermute(pair, "x", [(i, (i + k) % fan_x) for i in range(fan_x)])
        weights.append(pair)
    marks = pl.pallas_call(
        lambda *refs: marks_kernel(shards, rows, *refs),
        name="marks",
        out_shape=jax.ShapeDtypeStruct((2 * shards, chans), F32),
        in_specs=[SM], out_specs=VM,
        compiler_params=small,
        cost_estimate=cost(100_000, 20_000),
    )(segments)
    pay, taps = pl.pallas_call(
        finish_kernel,
        name="finish",
        out_shape=(
            jax.ShapeDtypeStruct((fan_y, rows, chans), BF16),
            jax.ShapeDtypeStruct((modes, chans), F32),
        ),
        in_specs=[VM] * 7, out_specs=(HB, VM),
        scratch_shapes=[pltpu.VMEM((modes, chans), F32), pltpu.VMEM((rows, chans), BF16), sem((fan_y,))],
        compiler_params=small,
        cost_estimate=cost(10_000_000, 1_000_000),
    )(heads_in, marks, residues, decay_rate, base, parts, first)
    pay_in = lax.all_to_all(pay, "y", 0, 0)
    for n in range(4):
        taps = taps + lax.ppermute(taps, "z", [(i, i ^ (1 << n)) for i in range(shards)])
    split = pl.pallas_call(
        product_kernel,
        name="product",
        out_shape=jax.ShapeDtypeStruct((2 * fan_x, rows, feats), BF16),
        in_specs=[VM] * (1 + fan_x), out_specs=VM,
        scratch_shapes=[pltpu.VMEM((rows, depth), BF16)],
        compiler_params=small,
        cost_estimate=cost(4 * rows * depth * fan_x * feats, 4_000_000),
    )(pay_in, *weights)
    split_in = lax.all_to_all(split, ("x", "c"), 0, 0)
    d_input = pl.pallas_call(
        sum_kernel,
        name="total",
        out_shape=jax.ShapeDtypeStruct((rows, feats), BF16),
        in_specs=[VM], out_specs=VM,
        compiler_params=small,
        cost_estimate=cost(1_000_000, 900_000),
    )(split_in)
    return d_input, taps


def solution(mesh):
    grid = (16, 4, 8, 2)
    fine = Mesh(mesh.devices.reshape(grid), ("z", "x", "y", "c"))
    head = ("x", "y", "c")
    return jax.shard_map(
        device,
        mesh=fine,
        in_specs=(P("z", head), P("z", head), P(None, head), P(None, head), P(), P(head, None)),
        out_specs=(P("z", head), P(None, head)),
        check_vma=False,
    )
```

```python
import jax
import jax.numpy as jnp
from jax import lax
from jax.experimental import pallas as pl
from jax.experimental.pallas import tpu as pltpu
from jax.sharding import Mesh, PartitionSpec as P


LANES = 128
SUB = 8
F32 = jnp.float32
BF16 = jnp.bfloat16

VM = pl.BlockSpec(memory_space=pltpu.VMEM)
SM = pl.BlockSpec(memory_space=pltpu.SMEM)
HB = pl.BlockSpec(memory_space=pl.ANY)


def scan_kernel(
    shards, seg_ref, g_ref, x_ref, res_ref, rate_ref,
    ends_ref, base_ref, gf, xf, prod, end_v, end_sem,
):
    rows = g_ref.shape[0]
    base = lax.axis_index("z") * rows
    gf[...] = g_ref[...].astype(F32)
    xf[...] = x_ref[...].astype(F32)
    decay = jnp.exp(-rate_ref[...])
    d0, d1 = decay[:SUB], decay[SUB:]
    r0, r1 = res_ref[:SUB], res_ref[SUB:]
    zero = jnp.zeros((SUB, LANES), F32)
    one = jnp.ones((SUB, LANES), F32)

    def block(i, carry):
        a0, a1, f0, f1, g0, g1, c0, c1, nxt = carry
        top = rows - 16 * (i + 1)
        for k in range(15, -1, -1):
            t = top + k
            seg = seg_ref[base + t]
            link = jnp.where(seg == nxt, 1.0, 0.0).astype(F32)
            nxt = seg
            e0, e1 = d0 * link, d1 * link
            g = row(gf, t)
            x = row(xf, t)
            a0 = g + e0 * a0
            a1 = g + e1 * a1
            g0 = e0 * g0
            g1 = e1 * g1
            f0 = f0 + x * a0
            f1 = f1 + x * a1
            c0 = c0 + x * g0
            c1 = c1 + x * g1
            prod[pl.ds(pl.multiple_of(t * SUB, SUB), SUB), :] = r0 * a0 + r1 * a1
        return a0, a1, f0, f1, g0, g1, c0, c1, nxt

    init = (zero, zero, zero, zero, one, one, zero, zero, seg_ref[base + rows - 1])
    a0, a1, f0, f1, _, _, c0, c1, _ = lax.fori_loop(0, rows // 16, block, init)
    for n, pair in enumerate(((a0, a1), (f0, f1), (c0, c1))):
        end_v[16 * n : 16 * n + 16] = jnp.concatenate(pair, axis=0).astype(BF16)
    ends = [pltpu.make_async_copy(end_v, ends_ref.at[i], end_sem.at[i]) for i in range(shards)]
    for c in ends:
        c.start()

    def fold(i, _):
        at = pl.multiple_of(i * 16, 16)
        total = prod[pl.ds(at * SUB, 16, stride=SUB), :]
        for k in range(1, SUB):
            total = total + prod[pl.ds(at * SUB + k, 16, stride=SUB), :]
        base_ref[pl.ds(at, 16), :] = total
        return 0

    lax.fori_loop(0, rows // 16, fold, 0)
    for c in ends:
        c.wait()


def sort_kernel(shards, rows, fan_x, fan_y, seg_ref, w_ref, *refs):
    outs, (marks_ref, first_ref, out_sem) = refs[:fan_x], refs[fan_x:]
    feats = w_ref.shape[0]
    width = w_ref.shape[1] // (2 * fan_x * fan_y)
    mine = lax.axis_index("c")
    here = lax.axis_index("x")
    cuts = []
    for k in reversed(range(fan_x)):
        to = lax.rem(here + k, fan_x)
        for y in range(fan_y):
            for other in range(2):
                core = 1 - mine if other else mine
                at = pl.multiple_of(((to * fan_y + y) * 2 + core) * width, width)
                cuts.append(
                    pltpu.make_async_copy(
                        w_ref.at[:, pl.ds(at, width)],
                        outs[k].at[pl.ds(other * feats, feats), pl.ds(y * width, width)],
                        out_sem.at[(k * fan_y + y) * 2 + other],
                    )
                )
    for c in cuts:
        c.start()
    for i in range(shards):
        begin = seg_ref[i * rows]
        end = seg_ref[i * rows + rows - 1]
        whole = jnp.where(begin == end, 1.0, 0.0).astype(F32)
        marks_ref[pl.ds(i, 1), :] = jnp.full((1, LANES), whole, F32)
        if i + 1 < shards:
            on = jnp.where(end == seg_ref[(i + 1) * rows], 1.0, 0.0).astype(F32)
        else:
            on = jnp.float32(0.0)
        marks_ref[pl.ds(shards + i, 1), :] = jnp.full((1, LANES), on, F32)
    start = lax.axis_index("z") * rows
    last = seg_ref[start + rows - 1]

    def halve(_, span):
        low, high = span
        mid = (low + high) // 2
        inside = seg_ref[start + mid] == last
        return jnp.where(inside, low, mid + 1), jnp.where(inside, mid, high)

    first, _ = lax.fori_loop(0, rows.bit_length(), halve, (jnp.int32(0), jnp.int32(rows - 1)))
    first_ref[...] = jnp.full((SUB, LANES), first, jnp.int32)
    for c in cuts:
        c.wait()


def row(ref, at):
    return ref[pl.ds(at, SUB, stride=0), :]


def chain(ends_ref, marks_ref, rate, rows, visit):
    shards = ends_ref.shape[0]
    leap = jnp.exp(-float(rows) * rate)
    state = jnp.zeros(leap.shape, F32)
    modes = leap.shape[0]
    for i in range(shards - 1, -1, -1):
        visit(i, state)
        if i:
            whole = marks_ref[pl.ds(i, 1), :]
            on = marks_ref[pl.ds(shards + i - 1, 1), :]
            state = on * (ends_ref[i, :modes].astype(F32) + whole * (leap * state))


def taps_kernel(rows, ends_ref, marks_ref, rate_ref, out_ref):
    modes = rate_ref.shape[0]
    total = [jnp.zeros(rate_ref.shape, F32)]

    def visit(i, state):
        own = ends_ref[i, modes : 2 * modes].astype(F32)
        gain = ends_ref[i, 2 * modes :].astype(F32)
        total[0] = total[0] + (own + gain * state)

    chain(ends_ref, marks_ref, rate_ref[...], rows, visit)
    out_ref[...] = total[0]


def finish_kernel(
    ends_ref, marks_ref, res_ref, rate_ref, base_ref, first_ref, pay_ref, amp_v, pay_v, pay_sem
):
    rows = base_ref.shape[0]
    modes = res_ref.shape[0]
    me = lax.axis_index("z")
    own = [jnp.zeros(rate_ref.shape, F32)]

    def visit(i, state):
        own[0] = jnp.where(me == i, state, own[0])

    chain(ends_ref, marks_ref, rate_ref[...], rows, visit)
    amp_v[...] = own[0] * res_ref[...]
    first = first_ref[...]
    place = lax.broadcasted_iota(jnp.int32, (SUB, LANES), 0)
    back = (SUB - place).astype(F32)
    steps, terms = [], []
    for m in range(modes):
        rate = row(rate_ref, m)
        steps.append(jnp.exp(rate * -float(SUB)))
        terms.append(row(amp_v, m) * jnp.exp(rate * -back))

    def tokens(i, terms):
        terms = list(terms)
        at = pl.multiple_of(rows - 16 * (i + 1), 16)
        halves = []
        for h in (1, 0):
            tree = list(terms)
            while len(tree) > 1:
                tree = [tree[k] + tree[k + 1] for k in range(0, len(tree), 2)]
            halves.append(jnp.where(place + (at + SUB * h) >= first, tree[0], 0.0))
            terms = [a * b for a, b in zip(terms, steps)]
        carry = jnp.concatenate([halves[1], halves[0]], axis=0)
        pay_v[pl.ds(at, 16), :] = (base_ref[pl.ds(at, 16), :] + carry).astype(BF16)
        return tuple(terms)

    lax.fori_loop(0, rows // 16, tokens, tuple(terms))
    pays = [
        pltpu.make_async_copy(pay_v, pay_ref.at[i], pay_sem.at[i]) for i in range(pay_ref.shape[0])
    ]
    for c in pays:
        c.start()
    for c in pays:
        c.wait()


def product_kernel(fan_x, pay_ref, own_ref, got_ref, out_ref, conv):
    mine = lax.axis_index("c")
    here = lax.axis_index("x")
    for y in range(pay_ref.shape[0]):
        conv[:, y * LANES : (y + 1) * LANES] = pay_ref[y]
    for core, w_ref in ((mine, own_ref), (1 - mine, got_ref)):
        for k in range(0, fan_x, 2):
            pair = lax.dot_general(
                conv[...], w_ref[k * LANES : (k + 2) * LANES, :],
                (((1,), (1,)), ((), ())), preferred_element_type=F32,
            )
            for n in range(2):
                to = 2 * lax.rem(here + fan_x - k - n, fan_x) + core
                out_ref[to] = pair[:, n * LANES : (n + 1) * LANES].astype(BF16)


def sum_kernel(parts_ref, out_ref):
    total = parts_ref[0].astype(F32)
    for i in range(1, parts_ref.shape[0]):
        total = total + parts_ref[i].astype(F32)
    out_ref[...] = total.astype(BF16)


def cost(flops, nbytes):
    return pl.CostEstimate(flops=flops, bytes_accessed=nbytes, transcendentals=0)


def device(out_grad, conv_input, residues, decay_rate, segments, w_in):
    shards, fan_x, fan_y = (lax.axis_size(n) for n in ("z", "x", "y"))
    rows, chans = out_grad.shape
    modes = residues.shape[0]
    feats, depth = w_in.shape[0], w_in.shape[1] // (2 * fan_x)
    sem = pltpu.SemaphoreType.DMA
    whole = pltpu.CompilerParams(vmem_limit_bytes=67_000_000)
    small = pltpu.CompilerParams(vmem_limit_bytes=16 * 2**20)
    ends, base = pl.pallas_call(
        lambda *refs: scan_kernel(shards, *refs),
        name="scan",
        out_shape=(
            jax.ShapeDtypeStruct((shards, 3 * modes, chans), BF16),
            jax.ShapeDtypeStruct((rows, chans), F32),
        ),
        in_specs=[SM, VM, VM, VM, VM],
        out_specs=(HB, VM),
        scratch_shapes=[
            pltpu.VMEM((rows, chans), F32), pltpu.VMEM((rows, chans), F32),
            pltpu.VMEM((rows * SUB, chans), F32), pltpu.VMEM((3 * modes, chans), BF16),
            sem((shards,)),
        ],
        compiler_params=whole,
        cost_estimate=cost(10_000_000, 8_000_000),
    )(segments, out_grad, conv_input, residues, decay_rate)

    ends_in = lax.all_to_all(ends, "z", 0, 0)
    *cuts, marks, first = pl.pallas_call(
        lambda *refs: sort_kernel(shards, rows, fan_x, fan_y, *refs),
        name="sort",
        out_shape=(
            *(jax.ShapeDtypeStruct((2 * feats, depth), BF16) for _ in range(fan_x)),
            jax.ShapeDtypeStruct((2 * shards, chans), F32),
            jax.ShapeDtypeStruct((SUB, chans), jnp.int32),
        ),
        in_specs=[SM, pl.BlockSpec(memory_space=pltpu.HBM)],
        out_specs=(VM,) * (fan_x + 2),
        scratch_shapes=[sem((2 * fan_x * fan_y,))],
        compiler_params=small,
        cost_estimate=cost(100_000, 4_000_000),
    )(segments, w_in)
    for k in (1, 3, 2):
        cuts[k] = lax.ppermute(cuts[k], "x", [(i, (i + k) % fan_x) for i in range(fan_x)])
    pay = pl.pallas_call(
        finish_kernel,
        name="finish",
        out_shape=jax.ShapeDtypeStruct((fan_y, rows, chans), BF16),
        in_specs=[VM] * 6, out_specs=HB,
        scratch_shapes=[
            pltpu.VMEM((modes, chans), F32), pltpu.VMEM((rows, chans), BF16), sem((fan_y,)),
        ],
        compiler_params=small,
        cost_estimate=cost(10_000_000, 1_000_000),
    )(ends_in, marks, residues, decay_rate, base, first)
    pay_in = lax.all_to_all(pay, "y", 0, 0)
    own = jnp.concatenate([a[:feats] for a in cuts], axis=0)
    give = jnp.concatenate([a[feats:] for a in cuts], axis=0)
    got = lax.ppermute(give, "c", [(0, 1), (1, 0)])
    split = pl.pallas_call(
        lambda *refs: product_kernel(fan_x, *refs),
        name="product",
        out_shape=jax.ShapeDtypeStruct((2 * fan_x, rows, feats), BF16),
        in_specs=[VM] * 3, out_specs=VM,
        scratch_shapes=[pltpu.VMEM((rows, depth), BF16)],
        compiler_params=small,
        cost_estimate=cost(4 * rows * depth * fan_x * feats, 4_000_000),
    )(pay_in, own, got)
    split_in = lax.all_to_all(split, ("x", "c"), 0, 0)
    taps = pl.pallas_call(
        lambda *refs: taps_kernel(rows, *refs),
        name="taps",
        out_shape=jax.ShapeDtypeStruct((modes, chans), F32),
        in_specs=[VM] * 3, out_specs=VM,
        compiler_params=small,
        cost_estimate=cost(1_000_000, 300_000),
    )(ends_in, marks, decay_rate)
    d_input = pl.pallas_call(
        sum_kernel,
        name="total",
        out_shape=jax.ShapeDtypeStruct((rows, feats), BF16),
        in_specs=[VM], out_specs=VM,
        compiler_params=small,
        cost_estimate=cost(1_000_000, 900_000),
    )(split_in)
    return d_input, taps


def solution(mesh):
    grid = (16, 4, 8, 2)
    fine = Mesh(mesh.devices.reshape(grid), ("z", "x", "y", "c"))
    head = ("x", "y", "c")
    return jax.shard_map(
        device,
        mesh=fine,
        in_specs=(P("z", head), P("z", head), P(None, head), P(None, head), P(), P(head, None)),
        out_specs=(P("z", head), P(None, head)),
        check_vma=False,
    )
```

```python
import jax
import jax.numpy as jnp
from jax import lax
from jax.experimental import pallas as pl
from jax.experimental.pallas import tpu as pltpu
from jax.sharding import Mesh, PartitionSpec as P


LANES = 128
SUB = 8
F32 = jnp.float32
BF16 = jnp.bfloat16

VM = pl.BlockSpec(memory_space=pltpu.VMEM)
SM = pl.BlockSpec(memory_space=pltpu.SMEM)
HB = pl.BlockSpec(memory_space=pl.ANY)


def scan_kernel(
    shards, fan_x, fan_y, seg_ref, g_ref, x_ref, res_ref, rate_ref, w_ref,
    ends_ref, base_ref, *refs
):
    outs, (gf, xf, prod, end_v, w_v, w_sem, cut_sem, end_sem) = refs[:fan_x], refs[fan_x:]
    rows = g_ref.shape[0]
    base = lax.axis_index("z") * rows
    w_in = pltpu.make_async_copy(w_ref, w_v, w_sem)
    w_in.start()
    gf[...] = g_ref[...].astype(F32)
    xf[...] = x_ref[...].astype(F32)
    decay = jnp.exp(-rate_ref[...])
    d0, d1 = decay[:SUB], decay[SUB:]
    r0, r1 = res_ref[:SUB], res_ref[SUB:]
    zero = jnp.zeros((SUB, LANES), F32)
    one = jnp.ones((SUB, LANES), F32)

    def block(i, carry):
        a0, a1, f0, f1, g0, g1, c0, c1, nxt = carry
        top = rows - 16 * (i + 1)
        for k in range(15, -1, -1):
            t = top + k
            seg = seg_ref[base + t]
            link = jnp.where(seg == nxt, 1.0, 0.0).astype(F32)
            nxt = seg
            e0, e1 = d0 * link, d1 * link
            g = row(gf, t)
            x = row(xf, t)
            a0 = g + e0 * a0
            a1 = g + e1 * a1
            g0 = e0 * g0
            g1 = e1 * g1
            f0 = f0 + x * a0
            f1 = f1 + x * a1
            c0 = c0 + x * g0
            c1 = c1 + x * g1
            prod[pl.ds(pl.multiple_of(t * SUB, SUB), SUB), :] = r0 * a0 + r1 * a1
        return a0, a1, f0, f1, g0, g1, c0, c1, nxt

    init = (zero, zero, zero, zero, one, one, zero, zero, seg_ref[base + rows - 1])
    half = lax.fori_loop(0, rows // 32, block, init)
    w_in.wait()
    feats = w_v.shape[0]
    width = w_v.shape[1] // (2 * fan_x * fan_y)
    mine = lax.axis_index("c")
    here = lax.axis_index("x")
    cuts = []
    for k in range(fan_x):
        to = lax.rem(here + k, fan_x)
        for y in range(fan_y):
            for other in range(2):
                core = 1 - mine if other else mine
                at = pl.multiple_of(((to * fan_y + y) * 2 + core) * width, width)
                cuts.append(
                    pltpu.make_async_copy(
                        w_v.at[:, pl.ds(at, width)],
                        outs[k].at[pl.ds(other * feats, feats), pl.ds(y * width, width)],
                        cut_sem.at[(k * fan_y + y) * 2 + other],
                    )
                )
    for c in cuts:
        c.start()
    a0, a1, f0, f1, _, _, c0, c1, _ = lax.fori_loop(rows // 32, rows // 16, block, half)
    state = jnp.concatenate((a0, a1), axis=0)
    high = state.astype(BF16)
    end_v[:16] = high
    end_v[16:32] = (state - high.astype(F32)).astype(BF16)
    end_v[32:48] = jnp.concatenate((f0, f1), axis=0).astype(BF16)
    end_v[48:] = jnp.concatenate((c0, c1), axis=0).astype(BF16)
    ends = [pltpu.make_async_copy(end_v, ends_ref.at[i], end_sem.at[i]) for i in range(shards)]
    for c in ends:
        c.start()

    def fold(i, _):
        at = pl.multiple_of(i * 16, 16)
        total = prod[pl.ds(at * SUB, 16, stride=SUB), :]
        for k in range(1, SUB):
            total = total + prod[pl.ds(at * SUB + k, 16, stride=SUB), :]
        base_ref[pl.ds(at, 16), :] = total
        return 0

    lax.fori_loop(0, rows // 16, fold, 0)
    for c in cuts + ends:
        c.wait()


def marks_kernel(shards, rows, seg_ref, base_ref, marks_ref, first_ref, same_ref):
    same_ref[...] = base_ref[...]
    for i in range(shards):
        begin = seg_ref[i * rows]
        end = seg_ref[i * rows + rows - 1]
        whole = jnp.where(begin == end, 1.0, 0.0).astype(F32)
        marks_ref[pl.ds(i, 1), :] = jnp.full((1, LANES), whole, F32)
        if i + 1 < shards:
            on = jnp.where(end == seg_ref[(i + 1) * rows], 1.0, 0.0).astype(F32)
        else:
            on = jnp.float32(0.0)
        marks_ref[pl.ds(shards + i, 1), :] = jnp.full((1, LANES), on, F32)
    start = lax.axis_index("z") * rows
    last = seg_ref[start + rows - 1]

    def halve(_, span):
        low, high = span
        mid = (low + high) // 2
        inside = seg_ref[start + mid] == last
        return jnp.where(inside, low, mid + 1), jnp.where(inside, mid, high)

    first, _ = lax.fori_loop(0, rows.bit_length(), halve, (jnp.int32(0), jnp.int32(rows - 1)))
    first_ref[...] = jnp.full((SUB, LANES), first, jnp.int32)


def row(ref, at):
    return ref[pl.ds(at, SUB, stride=0), :]


def chain(ends_ref, marks_ref, rate, rows, visit):
    shards = ends_ref.shape[0]
    leap = jnp.exp(-float(rows) * rate)
    state = jnp.zeros(leap.shape, F32)
    modes = leap.shape[0]
    for i in range(shards - 1, -1, -1):
        visit(i, state)
        if i:
            whole = marks_ref[pl.ds(i, 1), :]
            on = marks_ref[pl.ds(shards + i - 1, 1), :]
            head = ends_ref[i, :modes].astype(F32) + ends_ref[i, modes : 2 * modes].astype(F32)
            state = on * (head + whole * (leap * state))


def taps_kernel(rows, ends_ref, marks_ref, rate_ref, out_ref):
    modes = rate_ref.shape[0]
    total = [jnp.zeros(rate_ref.shape, F32)]

    def visit(i, state):
        own = ends_ref[i, 2 * modes : 3 * modes].astype(F32)
        gain = ends_ref[i, 3 * modes :].astype(F32)
        total[0] = total[0] + (own + gain * state)

    chain(ends_ref, marks_ref, rate_ref[...], rows, visit)
    out_ref[...] = total[0]


def finish_kernel(
    ends_ref, marks_ref, res_ref, rate_ref, base_ref, first_ref, pay_ref, amp_v, pay_v, pay_sem
):
    rows = base_ref.shape[0]
    modes = res_ref.shape[0]
    me = lax.axis_index("z")
    own = [jnp.zeros(rate_ref.shape, F32)]

    def visit(i, state):
        own[0] = jnp.where(me == i, state, own[0])

    chain(ends_ref, marks_ref, rate_ref[...], rows, visit)
    amp_v[...] = own[0] * res_ref[...]
    first = first_ref[...]
    place = lax.broadcasted_iota(jnp.int32, (SUB, LANES), 0)
    back = (SUB - place).astype(F32)
    steps, terms = [], []
    for m in range(modes):
        rate = row(rate_ref, m)
        steps.append(jnp.exp(rate * -float(SUB)))
        terms.append(row(amp_v, m) * jnp.exp(rate * -back))

    def tokens(i, terms):
        terms = list(terms)
        at = pl.multiple_of(rows - 16 * (i + 1), 16)
        halves = []
        for h in (1, 0):
            tree = list(terms)
            while len(tree) > 1:
                tree = [tree[k] + tree[k + 1] for k in range(0, len(tree), 2)]
            halves.append(jnp.where(place + (at + SUB * h) >= first, tree[0], 0.0))
            terms = [a * b for a, b in zip(terms, steps)]
        carry = jnp.concatenate([halves[1], halves[0]], axis=0)
        pay_v[pl.ds(at, 16), :] = (base_ref[pl.ds(at, 16), :] + carry).astype(BF16)
        return tuple(terms)

    lax.fori_loop(0, rows // 16, tokens, tuple(terms))
    pays = [
        pltpu.make_async_copy(pay_v, pay_ref.at[i], pay_sem.at[i]) for i in range(pay_ref.shape[0])
    ]
    for c in pays:
        c.start()
    for c in pays:
        c.wait()


def product_kernel(fan_x, pay_ref, own_ref, got_ref, out_ref, conv):
    mine = lax.axis_index("c")
    here = lax.axis_index("x")
    for y in range(pay_ref.shape[0]):
        conv[:, y * LANES : (y + 1) * LANES] = pay_ref[y]
    for core, w_ref in ((mine, own_ref), (1 - mine, got_ref)):
        for k in range(0, fan_x, 2):
            pair = lax.dot_general(
                conv[...], w_ref[k * LANES : (k + 2) * LANES, :],
                (((1,), (1,)), ((), ())), preferred_element_type=F32,
            )
            for n in range(2):
                to = 2 * lax.rem(here + fan_x - k - n, fan_x) + core
                out_ref[to] = pair[:, n * LANES : (n + 1) * LANES].astype(BF16)


def sum_kernel(parts_ref, out_ref):
    total = parts_ref[0].astype(F32)
    for i in range(1, parts_ref.shape[0]):
        total = total + parts_ref[i].astype(F32)
    out_ref[...] = total.astype(BF16)


def cost(flops, nbytes):
    return pl.CostEstimate(flops=flops, bytes_accessed=nbytes, transcendentals=0)


def device(out_grad, conv_input, residues, decay_rate, segments, w_in):
    shards, fan_x, fan_y = (lax.axis_size(n) for n in ("z", "x", "y"))
    rows, chans = out_grad.shape
    modes = residues.shape[0]
    feats, depth = w_in.shape[0], w_in.shape[1] // (2 * fan_x)
    sem = pltpu.SemaphoreType.DMA
    whole = pltpu.CompilerParams(vmem_limit_bytes=67_000_000)
    small = pltpu.CompilerParams(vmem_limit_bytes=16 * 2**20)
    ends, base, *cuts = pl.pallas_call(
        lambda *refs: scan_kernel(shards, fan_x, fan_y, *refs),
        name="scan",
        out_shape=(
            jax.ShapeDtypeStruct((shards, 4 * modes, chans), BF16),
            jax.ShapeDtypeStruct((rows, chans), F32),
            *(jax.ShapeDtypeStruct((2 * feats, depth), BF16) for _ in range(fan_x)),
        ),
        in_specs=[SM, VM, VM, VM, VM, HB],
        out_specs=(HB, VM, *(HB,) * fan_x),
        scratch_shapes=[
            pltpu.VMEM((rows, chans), F32), pltpu.VMEM((rows, chans), F32),
            pltpu.VMEM((rows * SUB, chans), F32), pltpu.VMEM((4 * modes, chans), BF16),
            pltpu.VMEM(w_in.shape, BF16), sem(()), sem((2 * fan_x * fan_y,)), sem((shards,)),
        ],
        compiler_params=whole,
        cost_estimate=cost(10_000_000, 8_000_000),
    )(segments, out_grad, conv_input, residues, decay_rate, w_in)

    ends_in = lax.all_to_all(ends, "z", 0, 0)
    marks, first, base = pl.pallas_call(
        lambda *refs: marks_kernel(shards, rows, *refs),
        name="marks",
        out_shape=(
            jax.ShapeDtypeStruct((2 * shards, chans), F32),
            jax.ShapeDtypeStruct((SUB, chans), jnp.int32),
            jax.ShapeDtypeStruct((rows, chans), F32),
        ),
        in_specs=[SM, VM], out_specs=(VM, VM, VM),
        compiler_params=small,
        cost_estimate=cost(100_000, 100_000),
    )(segments, base)
    for k in (1, 3, 2):
        cuts[k] = lax.ppermute(cuts[k], "x", [(i, (i + k) % fan_x) for i in range(fan_x)])
    pay = pl.pallas_call(
        finish_kernel,
        name="finish",
        out_shape=jax.ShapeDtypeStruct((fan_y, rows, chans), BF16),
        in_specs=[VM] * 6, out_specs=HB,
        scratch_shapes=[
            pltpu.VMEM((modes, chans), F32), pltpu.VMEM((rows, chans), BF16), sem((fan_y,)),
        ],
        compiler_params=small,
        cost_estimate=cost(10_000_000, 1_000_000),
    )(ends_in, marks, residues, decay_rate, base, first)
    pay_in = lax.all_to_all(pay, "y", 0, 0)
    own = jnp.concatenate([a[:feats] for a in cuts], axis=0)
    give = jnp.concatenate([a[feats:] for a in cuts], axis=0)
    got = lax.ppermute(give, "c", [(0, 1), (1, 0)])
    split = pl.pallas_call(
        lambda *refs: product_kernel(fan_x, *refs),
        name="product",
        out_shape=jax.ShapeDtypeStruct((2 * fan_x, rows, feats), BF16),
        in_specs=[VM] * 3, out_specs=VM,
        scratch_shapes=[pltpu.VMEM((rows, depth), BF16)],
        compiler_params=small,
        cost_estimate=cost(4 * rows * depth * fan_x * feats, 4_000_000),
    )(pay_in, own, got)
    split_in = lax.all_to_all(split, ("x", "c"), 0, 0)
    taps = pl.pallas_call(
        lambda *refs: taps_kernel(rows, *refs),
        name="taps",
        out_shape=jax.ShapeDtypeStruct((modes, chans), F32),
        in_specs=[VM] * 3, out_specs=VM,
        compiler_params=small,
        cost_estimate=cost(1_000_000, 300_000),
    )(ends_in, marks, decay_rate)
    d_input = pl.pallas_call(
        sum_kernel,
        name="total",
        out_shape=jax.ShapeDtypeStruct((rows, feats), BF16),
        in_specs=[VM], out_specs=VM,
        compiler_params=small,
        cost_estimate=cost(1_000_000, 900_000),
    )(split_in)
    return d_input, taps


def solution(mesh):
    grid = (16, 4, 8, 2)
    fine = Mesh(mesh.devices.reshape(grid), ("z", "x", "y", "c"))
    head = ("x", "y", "c")
    return jax.shard_map(
        device,
        mesh=fine,
        in_specs=(P("z", head), P("z", head), P(None, head), P(None, head), P(), P(head, None)),
        out_specs=(P("z", head), P(None, head)),
        check_vma=False,
    )
```

```python
import jax
import jax.numpy as jnp
from jax import lax
from jax.experimental import pallas as pl
from jax.experimental.pallas import tpu as pltpu
from jax.sharding import Mesh, PartitionSpec as P


LANES = 128
SUB = 8
F32 = jnp.float32
BF16 = jnp.bfloat16

VM = pl.BlockSpec(memory_space=pltpu.VMEM)
SM = pl.BlockSpec(memory_space=pltpu.SMEM)
HB = pl.BlockSpec(memory_space=pl.ANY)


def scan_kernel(
    shards, seg_ref, g_ref, x_ref, res_ref, rate_ref,
    ends_ref, base_ref, gf, xf, prod, end_v, end_sem,
):
    rows = g_ref.shape[0]
    base = lax.axis_index("z") * rows
    gf[...] = g_ref[...].astype(F32)
    xf[...] = x_ref[...].astype(F32)
    decay = jnp.exp(-rate_ref[...])
    d0, d1 = decay[:SUB], decay[SUB:]
    r0, r1 = res_ref[:SUB], res_ref[SUB:]
    zero = jnp.zeros((SUB, LANES), F32)
    one = jnp.ones((SUB, LANES), F32)

    def block(i, carry):
        a0, a1, f0, f1, g0, g1, c0, c1, nxt = carry
        top = rows - 16 * (i + 1)
        for k in range(15, -1, -1):
            t = top + k
            seg = seg_ref[base + t]
            link = jnp.where(seg == nxt, 1.0, 0.0).astype(F32)
            nxt = seg
            e0, e1 = d0 * link, d1 * link
            g = row(gf, t)
            x = row(xf, t)
            a0 = g + e0 * a0
            a1 = g + e1 * a1
            g0 = e0 * g0
            g1 = e1 * g1
            f0 = f0 + x * a0
            f1 = f1 + x * a1
            c0 = c0 + x * g0
            c1 = c1 + x * g1
            prod[pl.ds(pl.multiple_of(t * SUB, SUB), SUB), :] = r0 * a0 + r1 * a1
        return a0, a1, f0, f1, g0, g1, c0, c1, nxt

    init = (zero, zero, zero, zero, one, one, zero, zero, seg_ref[base + rows - 1])
    a0, a1, f0, f1, _, _, c0, c1, _ = lax.fori_loop(0, rows // 16, block, init)
    for n, pair in enumerate(((a0, a1), (f0, f1), (c0, c1))):
        end_v[16 * n : 16 * n + 16] = jnp.concatenate(pair, axis=0).astype(BF16)
    ends = [pltpu.make_async_copy(end_v, ends_ref.at[i], end_sem.at[i]) for i in range(shards)]
    for c in ends:
        c.start()

    def fold(i, _):
        at = pl.multiple_of(i * 16, 16)
        total = prod[pl.ds(at * SUB, 16, stride=SUB), :]
        for k in range(1, SUB):
            total = total + prod[pl.ds(at * SUB + k, 16, stride=SUB), :]
        base_ref[pl.ds(at, 16), :] = total
        return 0

    lax.fori_loop(0, rows // 16, fold, 0)
    for c in ends:
        c.wait()


def start_cuts(ks, fan_x, fan_y, w_ref, outs, sem):
    feats = w_ref.shape[0]
    width = w_ref.shape[1] // (2 * fan_x * fan_y)
    mine = lax.axis_index("c")
    here = lax.axis_index("x")
    cuts = []
    for k, out in zip(ks, outs):
        to = lax.rem(here + k, fan_x)
        for y in range(fan_y):
            for other in range(2):
                core = 1 - mine if other else mine
                at = pl.multiple_of(((to * fan_y + y) * 2 + core) * width, width)
                cuts.append(
                    pltpu.make_async_copy(
                        w_ref.at[:, pl.ds(at, width)],
                        out.at[pl.ds(other * feats, feats), pl.ds(y * width, width)],
                        sem.at[len(cuts)],
                    )
                )
    for c in cuts:
        c.start()
    return cuts


def own_kernel(fan_x, fan_y, w_ref, out_ref, sem):
    for c in start_cuts((0,), fan_x, fan_y, w_ref, (out_ref,), sem):
        c.wait()


def sort_kernel(shards, rows, fan_x, fan_y, seg_ref, w_ref, *refs):
    outs, (marks_ref, first_ref, out_sem) = refs[: fan_x - 1], refs[fan_x - 1 :]
    cuts = start_cuts(range(1, fan_x), fan_x, fan_y, w_ref, outs, out_sem)
    for i in range(shards):
        begin = seg_ref[i * rows]
        end = seg_ref[i * rows + rows - 1]
        whole = jnp.where(begin == end, 1.0, 0.0).astype(F32)
        marks_ref[pl.ds(i, 1), :] = jnp.full((1, LANES), whole, F32)
        if i + 1 < shards:
            on = jnp.where(end == seg_ref[(i + 1) * rows], 1.0, 0.0).astype(F32)
        else:
            on = jnp.float32(0.0)
        marks_ref[pl.ds(shards + i, 1), :] = jnp.full((1, LANES), on, F32)
    start = lax.axis_index("z") * rows
    last = seg_ref[start + rows - 1]

    def halve(_, span):
        low, high = span
        mid = (low + high) // 2
        inside = seg_ref[start + mid] == last
        return jnp.where(inside, low, mid + 1), jnp.where(inside, mid, high)

    first, _ = lax.fori_loop(0, rows.bit_length(), halve, (jnp.int32(0), jnp.int32(rows - 1)))
    first_ref[...] = jnp.full((SUB, LANES), first, jnp.int32)
    for c in cuts:
        c.wait()


def row(ref, at):
    return ref[pl.ds(at, SUB, stride=0), :]


def chain(ends_ref, marks_ref, rate, rows, visit):
    shards = ends_ref.shape[0]
    leap = jnp.exp(-float(rows) * rate)
    state = jnp.zeros(leap.shape, F32)
    modes = leap.shape[0]
    for i in range(shards - 1, -1, -1):
        visit(i, state)
        if i:
            whole = marks_ref[pl.ds(i, 1), :]
            on = marks_ref[pl.ds(shards + i - 1, 1), :]
            state = on * (ends_ref[i, :modes].astype(F32) + whole * (leap * state))


def taps_kernel(rows, ends_ref, marks_ref, rate_ref, out_ref):
    modes = rate_ref.shape[0]
    total = [jnp.zeros(rate_ref.shape, F32)]

    def visit(i, state):
        own = ends_ref[i, modes : 2 * modes].astype(F32)
        gain = ends_ref[i, 2 * modes :].astype(F32)
        total[0] = total[0] + (own + gain * state)

    chain(ends_ref, marks_ref, rate_ref[...], rows, visit)
    out_ref[...] = total[0]


def finish_kernel(
    ends_ref, marks_ref, res_ref, rate_ref, base_ref, first_ref, pay_ref, amp_v, pay_v, pay_sem
):
    rows = base_ref.shape[0]
    modes = res_ref.shape[0]
    me = lax.axis_index("z")
    own = [jnp.zeros(rate_ref.shape, F32)]

    def visit(i, state):
        own[0] = jnp.where(me == i, state, own[0])

    chain(ends_ref, marks_ref, rate_ref[...], rows, visit)
    amp_v[...] = own[0] * res_ref[...]
    first = first_ref[...]
    place = lax.broadcasted_iota(jnp.int32, (SUB, LANES), 0)
    back = (SUB - place).astype(F32)
    steps, terms = [], []
    for m in range(modes):
        rate = row(rate_ref, m)
        steps.append(jnp.exp(rate * -float(SUB)))
        terms.append(row(amp_v, m) * jnp.exp(rate * -back))

    def tokens(i, terms):
        terms = list(terms)
        at = pl.multiple_of(rows - 16 * (i + 1), 16)
        halves = []
        for h in (1, 0):
            tree = list(terms)
            while len(tree) > 1:
                tree = [tree[k] + tree[k + 1] for k in range(0, len(tree), 2)]
            halves.append(jnp.where(place + (at + SUB * h) >= first, tree[0], 0.0))
            terms = [a * b for a, b in zip(terms, steps)]
        carry = jnp.concatenate([halves[1], halves[0]], axis=0)
        pay_v[pl.ds(at, 16), :] = (base_ref[pl.ds(at, 16), :] + carry).astype(BF16)
        return tuple(terms)

    lax.fori_loop(0, rows // 16, tokens, tuple(terms))
    pays = [
        pltpu.make_async_copy(pay_v, pay_ref.at[i], pay_sem.at[i]) for i in range(pay_ref.shape[0])
    ]
    for c in pays:
        c.start()
    for c in pays:
        c.wait()


def product_kernel(fan_x, pay_ref, own_ref, got_ref, keep_ref, give_ref, conv):
    for y in range(pay_ref.shape[0]):
        conv[:, y * LANES : (y + 1) * LANES] = pay_ref[y]
    for w_ref, out_ref in ((got_ref, give_ref), (own_ref, keep_ref)):
        for k in range(0, fan_x, 2):
            pair = lax.dot_general(
                conv[...], w_ref[k * LANES : (k + 2) * LANES, :],
                (((1,), (1,)), ((), ())), preferred_element_type=F32,
            )
            for n in range(2):
                part = pair[:, n * LANES : (n + 1) * LANES]
                out_ref[k + n] = part.astype(out_ref.dtype)


def join_kernel(keep_ref, got_ref, *out_refs):
    for k, out_ref in enumerate(out_refs):
        out_ref[...] = (keep_ref[k] + got_ref[k].astype(F32)).astype(out_ref.dtype)


def sum_kernel(own_ref, *refs):
    total = own_ref[...]
    for ref in refs[:-1]:
        total = total + ref[...].astype(F32)
    refs[-1][...] = total.astype(BF16)


def cost(flops, nbytes):
    return pl.CostEstimate(flops=flops, bytes_accessed=nbytes, transcendentals=0)


def device(out_grad, conv_input, residues, decay_rate, segments, w_in):
    shards, fan_x, fan_y = (lax.axis_size(n) for n in ("z", "x", "y"))
    rows, chans = out_grad.shape
    modes = residues.shape[0]
    feats, depth = w_in.shape[0], w_in.shape[1] // (2 * fan_x)
    sem = pltpu.SemaphoreType.DMA
    whole = pltpu.CompilerParams(vmem_limit_bytes=67_000_000)
    small = pltpu.CompilerParams(vmem_limit_bytes=16 * 2**20)
    ends, base = pl.pallas_call(
        lambda *refs: scan_kernel(shards, *refs),
        name="scan",
        out_shape=(
            jax.ShapeDtypeStruct((shards, 3 * modes, chans), BF16),
            jax.ShapeDtypeStruct((rows, chans), F32),
        ),
        in_specs=[SM, VM, VM, VM, VM],
        out_specs=(HB, VM),
        scratch_shapes=[
            pltpu.VMEM((rows, chans), F32), pltpu.VMEM((rows, chans), F32),
            pltpu.VMEM((rows * SUB, chans), F32), pltpu.VMEM((3 * modes, chans), BF16),
            sem((shards,)),
        ],
        compiler_params=whole,
        cost_estimate=cost(10_000_000, 8_000_000),
    )(segments, out_grad, conv_input, residues, decay_rate)

    ends_in = lax.all_to_all(ends, "z", 0, 0)
    *cuts, marks, first = pl.pallas_call(
        lambda *refs: sort_kernel(shards, rows, fan_x, fan_y, *refs),
        name="sort",
        out_shape=(
            *(jax.ShapeDtypeStruct((2 * feats, depth), BF16) for _ in range(fan_x - 1)),
            jax.ShapeDtypeStruct((2 * shards, chans), F32),
            jax.ShapeDtypeStruct((SUB, chans), jnp.int32),
        ),
        in_specs=[SM, pl.BlockSpec(memory_space=pltpu.HBM)],
        out_specs=(VM,) * (fan_x + 1),
        scratch_shapes=[sem((2 * (fan_x - 1) * fan_y,))],
        compiler_params=small,
        cost_estimate=cost(100_000, 4_000_000),
    )(segments, w_in)
    cuts = [None, *cuts]
    for k in (1, 3, 2):
        cuts[k] = lax.ppermute(cuts[k], "x", [(i, (i + k) % fan_x) for i in range(fan_x)])
    pay = pl.pallas_call(
        finish_kernel,
        name="finish",
        out_shape=jax.ShapeDtypeStruct((fan_y, rows, chans), BF16),
        in_specs=[VM] * 6, out_specs=HB,
        scratch_shapes=[
            pltpu.VMEM((modes, chans), F32), pltpu.VMEM((rows, chans), BF16), sem((fan_y,)),
        ],
        compiler_params=small,
        cost_estimate=cost(10_000_000, 1_000_000),
    )(ends_in, marks, residues, decay_rate, base, first)
    pay_in = lax.all_to_all(pay, "y", 0, 0)
    cuts[0] = pl.pallas_call(
        lambda *refs: own_kernel(fan_x, fan_y, *refs),
        name="own",
        out_shape=jax.ShapeDtypeStruct((2 * feats, depth), BF16),
        in_specs=[HB], out_specs=VM,
        scratch_shapes=[sem((2 * fan_y,))],
        compiler_params=small,
        cost_estimate=cost(100_000, 1_000_000),
    )(w_in)
    own = jnp.concatenate([a[:feats] for a in cuts], axis=0)
    give = jnp.concatenate([a[feats:] for a in cuts], axis=0)
    got = lax.ppermute(give, "c", [(0, 1), (1, 0)])
    keep, give = pl.pallas_call(
        lambda *refs: product_kernel(fan_x, *refs),
        name="product",
        out_shape=(
            jax.ShapeDtypeStruct((fan_x, rows, feats), F32),
            jax.ShapeDtypeStruct((fan_x, rows, feats), BF16),
        ),
        in_specs=[VM] * 3, out_specs=(VM, VM),
        scratch_shapes=[pltpu.VMEM((rows, depth), BF16)],
        compiler_params=small,
        cost_estimate=cost(4 * rows * depth * fan_x * feats, 4_000_000),
    )(pay_in, own, got)
    swapped = lax.ppermute(give, "c", [(0, 1), (1, 0)])
    taps = pl.pallas_call(
        lambda *refs: taps_kernel(rows, *refs),
        name="taps",
        out_shape=jax.ShapeDtypeStruct((modes, chans), F32),
        in_specs=[VM] * 3, out_specs=VM,
        compiler_params=small,
        cost_estimate=cost(1_000_000, 300_000),
    )(ends_in, marks, decay_rate)
    parts = pl.pallas_call(
        join_kernel,
        name="join",
        out_shape=tuple(
            jax.ShapeDtypeStruct((rows, feats), BF16 if k else F32) for k in range(fan_x)
        ),
        in_specs=[VM] * 2, out_specs=(VM,) * fan_x,
        compiler_params=small,
        cost_estimate=cost(1_000_000, 2_000_000),
    )(keep, swapped)
    parts = list(parts)
    for k in (1, 3, 2):
        parts[k] = lax.ppermute(parts[k], "x", [(i, (i - k) % fan_x) for i in range(fan_x)])
    d_input = pl.pallas_call(
        sum_kernel,
        name="total",
        out_shape=jax.ShapeDtypeStruct((rows, feats), BF16),
        in_specs=[VM] * fan_x, out_specs=VM,
        compiler_params=small,
        cost_estimate=cost(1_000_000, 900_000),
    )(*parts)
    return d_input, taps


def solution(mesh):
    grid = (16, 4, 8, 2)
    fine = Mesh(mesh.devices.reshape(grid), ("z", "x", "y", "c"))
    head = ("x", "y", "c")
    return jax.shard_map(
        device,
        mesh=fine,
        in_specs=(P("z", head), P("z", head), P(None, head), P(None, head), P(), P(head, None)),
        out_specs=(P("z", head), P(None, head)),
        check_vma=False,
    )
```

```python
import jax
import jax.numpy as jnp
from jax import lax
from jax.experimental import pallas as pl
from jax.experimental.pallas import tpu as pltpu
from jax.sharding import Mesh, PartitionSpec as P


LANES = 128
SUB = 8
F32 = jnp.float32
BF16 = jnp.bfloat16

VM = pl.BlockSpec(memory_space=pltpu.VMEM)
SM = pl.BlockSpec(memory_space=pltpu.SMEM)
HB = pl.BlockSpec(memory_space=pl.ANY)


def scan_kernel(
    shards, seg_ref, g_ref, x_ref, res_ref, rate_ref,
    ends_ref, base_ref, marks_ref, first_ref, gf, xf, prod, end_v, end_sem,
):
    rows = g_ref.shape[0]
    base = lax.axis_index("z") * rows
    gf[...] = g_ref[...].astype(F32)
    xf[...] = x_ref[...].astype(F32)
    decay = jnp.exp(-rate_ref[...])
    d0, d1 = decay[:SUB], decay[SUB:]
    r0, r1 = res_ref[:SUB], res_ref[SUB:]
    zero = jnp.zeros((SUB, LANES), F32)
    one = jnp.ones((SUB, LANES), F32)

    def block(i, carry):
        a0, a1, f0, f1, g0, g1, c0, c1, nxt = carry
        top = rows - 16 * (i + 1)
        for k in range(15, -1, -1):
            t = top + k
            seg = seg_ref[base + t]
            link = jnp.where(seg == nxt, 1.0, 0.0).astype(F32)
            nxt = seg
            e0, e1 = d0 * link, d1 * link
            g = row(gf, t)
            x = row(xf, t)
            a0 = g + e0 * a0
            a1 = g + e1 * a1
            g0 = e0 * g0
            g1 = e1 * g1
            f0 = f0 + x * a0
            f1 = f1 + x * a1
            c0 = c0 + x * g0
            c1 = c1 + x * g1
            prod[pl.ds(pl.multiple_of(t * SUB, SUB), SUB), :] = r0 * a0 + r1 * a1
        return a0, a1, f0, f1, g0, g1, c0, c1, nxt

    init = (zero, zero, zero, zero, one, one, zero, zero, seg_ref[base + rows - 1])
    a0, a1, f0, f1, _, _, c0, c1, _ = lax.fori_loop(0, rows // 16, block, init)
    for n, pair in enumerate(((a0, a1), (f0, f1), (c0, c1))):
        end_v[16 * n : 16 * n + 16] = jnp.concatenate(pair, axis=0).astype(BF16)
    ends = [pltpu.make_async_copy(end_v, ends_ref.at[i], end_sem.at[i]) for i in range(shards)]
    for c in ends:
        c.start()

    def fold(i, _):
        at = pl.multiple_of(i * 16, 16)
        total = prod[pl.ds(at * SUB, 16, stride=SUB), :]
        for k in range(1, SUB):
            total = total + prod[pl.ds(at * SUB + k, 16, stride=SUB), :]
        base_ref[pl.ds(at, 16), :] = total
        return 0

    lax.fori_loop(0, rows // 16, fold, 0)
    for i in range(shards):
        begin = seg_ref[i * rows]
        end = seg_ref[i * rows + rows - 1]
        whole = jnp.where(begin == end, 1.0, 0.0).astype(F32)
        marks_ref[pl.ds(i, 1), :] = jnp.full((1, LANES), whole, F32)
        if i + 1 < shards:
            on = jnp.where(end == seg_ref[(i + 1) * rows], 1.0, 0.0).astype(F32)
        else:
            on = jnp.float32(0.0)
        marks_ref[pl.ds(shards + i, 1), :] = jnp.full((1, LANES), on, F32)
    last = seg_ref[base + rows - 1]

    def halve(_, span):
        low, high = span
        mid = (low + high) // 2
        inside = seg_ref[base + mid] == last
        return jnp.where(inside, low, mid + 1), jnp.where(inside, mid, high)

    first, _ = lax.fori_loop(0, rows.bit_length(), halve, (jnp.int32(0), jnp.int32(rows - 1)))
    first_ref[...] = jnp.full((SUB, LANES), first, jnp.int32)
    for c in ends:
        c.wait()


def start_cuts(ks, fan_x, fan_y, w_ref, outs, sem):
    feats = w_ref.shape[0]
    width = w_ref.shape[1] // (2 * fan_x * fan_y)
    mine = lax.axis_index("c")
    here = lax.axis_index("x")
    cuts = []
    for k, out in zip(ks, outs):
        to = lax.rem(here + k, fan_x)
        for y in range(fan_y):
            for other in range(2):
                core = 1 - mine if other else mine
                at = pl.multiple_of(((to * fan_y + y) * 2 + core) * width, width)
                cuts.append(
                    pltpu.make_async_copy(
                        w_ref.at[:, pl.ds(at, width)],
                        out.at[pl.ds(other * feats, feats), pl.ds(y * width, width)],
                        sem.at[len(cuts)],
                    )
                )
    for c in cuts:
        c.start()
    return cuts


def own_kernel(fan_x, fan_y, w_ref, out_ref, sem):
    for c in start_cuts((0,), fan_x, fan_y, w_ref, (out_ref,), sem):
        c.wait()


def sort_kernel(fan_x, fan_y, w_ref, *refs):
    cuts = start_cuts(range(1, fan_x), fan_x, fan_y, w_ref, refs[:-1], refs[-1])
    for c in cuts:
        c.wait()


def row(ref, at):
    return ref[pl.ds(at, SUB, stride=0), :]


def chain(ends_ref, marks_ref, rate, rows, visit):
    shards = ends_ref.shape[0]
    leap = jnp.exp(-float(rows) * rate)
    state = jnp.zeros(leap.shape, F32)
    modes = leap.shape[0]
    for i in range(shards - 1, -1, -1):
        visit(i, state)
        if i:
            whole = marks_ref[pl.ds(i, 1), :]
            on = marks_ref[pl.ds(shards + i - 1, 1), :]
            state = on * (ends_ref[i, :modes].astype(F32) + whole * (leap * state))


def taps_kernel(rows, ends_ref, marks_ref, rate_ref, out_ref):
    modes = rate_ref.shape[0]
    total = [jnp.zeros(rate_ref.shape, F32)]

    def visit(i, state):
        own = ends_ref[i, modes : 2 * modes].astype(F32)
        gain = ends_ref[i, 2 * modes :].astype(F32)
        total[0] = total[0] + (own + gain * state)

    chain(ends_ref, marks_ref, rate_ref[...], rows, visit)
    out_ref[...] = total[0]


def finish_kernel(
    ends_ref, marks_ref, res_ref, rate_ref, base_ref, first_ref, pay_ref, amp_v, pay_v, pay_sem
):
    rows = base_ref.shape[0]
    modes = res_ref.shape[0]
    me = lax.axis_index("z")
    own = [jnp.zeros(rate_ref.shape, F32)]

    def visit(i, state):
        own[0] = jnp.where(me == i, state, own[0])

    chain(ends_ref, marks_ref, rate_ref[...], rows, visit)
    amp_v[...] = own[0] * res_ref[...]
    first = first_ref[...]
    place = lax.broadcasted_iota(jnp.int32, (SUB, LANES), 0)
    back = (SUB - place).astype(F32)
    steps, terms = [], []
    for m in range(modes):
        rate = row(rate_ref, m)
        steps.append(jnp.exp(rate * -float(SUB)))
        terms.append(row(amp_v, m) * jnp.exp(rate * -back))

    def tokens(i, terms):
        terms = list(terms)
        at = pl.multiple_of(rows - 16 * (i + 1), 16)
        halves = []
        for h in (1, 0):
            tree = list(terms)
            while len(tree) > 1:
                tree = [tree[k] + tree[k + 1] for k in range(0, len(tree), 2)]
            halves.append(jnp.where(place + (at + SUB * h) >= first, tree[0], 0.0))
            terms = [a * b for a, b in zip(terms, steps)]
        carry = jnp.concatenate([halves[1], halves[0]], axis=0)
        pay_v[pl.ds(at, 16), :] = (base_ref[pl.ds(at, 16), :] + carry).astype(BF16)
        return tuple(terms)

    lax.fori_loop(0, rows // 16, tokens, tuple(terms))
    pays = [
        pltpu.make_async_copy(pay_v, pay_ref.at[i], pay_sem.at[i]) for i in range(pay_ref.shape[0])
    ]
    for c in pays:
        c.start()
    for c in pays:
        c.wait()


def product_kernel(fan_x, pay_ref, own_ref, got_ref, keep_ref, give_ref, conv):
    for y in range(pay_ref.shape[0]):
        conv[:, y * LANES : (y + 1) * LANES] = pay_ref[y]
    for w_ref, out_ref in ((got_ref, give_ref), (own_ref, keep_ref)):
        for k in range(0, fan_x, 2):
            pair = lax.dot_general(
                conv[...], w_ref[k * LANES : (k + 2) * LANES, :],
                (((1,), (1,)), ((), ())), preferred_element_type=F32,
            )
            for n in range(2):
                part = pair[:, n * LANES : (n + 1) * LANES]
                out_ref[k + n] = part.astype(out_ref.dtype)


def join_kernel(keep_ref, got_ref, *out_refs):
    for k, out_ref in enumerate(out_refs):
        out_ref[...] = (keep_ref[k] + got_ref[k].astype(F32)).astype(out_ref.dtype)


def sum_kernel(own_ref, *refs):
    total = own_ref[...]
    for ref in refs[:-1]:
        total = total + ref[...].astype(F32)
    refs[-1][...] = total.astype(BF16)


def cost(flops, nbytes):
    return pl.CostEstimate(flops=flops, bytes_accessed=nbytes, transcendentals=0)


def device(out_grad, conv_input, residues, decay_rate, segments, w_in):
    shards, fan_x, fan_y = (lax.axis_size(n) for n in ("z", "x", "y"))
    rows, chans = out_grad.shape
    modes = residues.shape[0]
    feats, depth = w_in.shape[0], w_in.shape[1] // (2 * fan_x)
    sem = pltpu.SemaphoreType.DMA
    whole = pltpu.CompilerParams(vmem_limit_bytes=67_000_000)
    small = pltpu.CompilerParams(vmem_limit_bytes=16 * 2**20)
    ends, base, marks, first = pl.pallas_call(
        lambda *refs: scan_kernel(shards, *refs),
        name="scan",
        out_shape=(
            jax.ShapeDtypeStruct((shards, 3 * modes, chans), BF16),
            jax.ShapeDtypeStruct((rows, chans), F32),
            jax.ShapeDtypeStruct((2 * shards, chans), F32),
            jax.ShapeDtypeStruct((SUB, chans), jnp.int32),
        ),
        in_specs=[SM, VM, VM, VM, VM],
        out_specs=(HB, VM, VM, VM),
        scratch_shapes=[
            pltpu.VMEM((rows, chans), F32), pltpu.VMEM((rows, chans), F32),
            pltpu.VMEM((rows * SUB, chans), F32), pltpu.VMEM((3 * modes, chans), BF16),
            sem((shards,)),
        ],
        compiler_params=whole,
        cost_estimate=cost(10_000_000, 8_000_000),
    )(segments, out_grad, conv_input, residues, decay_rate)

    ends_in = lax.all_to_all(ends, "z", 0, 0)
    cuts = pl.pallas_call(
        lambda *refs: sort_kernel(fan_x, fan_y, *refs),
        name="sort",
        out_shape=tuple(jax.ShapeDtypeStruct((2 * feats, depth), BF16) for _ in range(fan_x - 1)),
        in_specs=[HB], out_specs=(VM,) * (fan_x - 1),
        scratch_shapes=[sem((2 * (fan_x - 1) * fan_y,))],
        compiler_params=small,
        cost_estimate=cost(100_000, 4_000_000),
    )(w_in)
    cuts = [None, *cuts]
    for k in (1, 3, 2):
        cuts[k] = lax.ppermute(cuts[k], "x", [(i, (i + k) % fan_x) for i in range(fan_x)])
    pay = pl.pallas_call(
        finish_kernel,
        name="finish",
        out_shape=jax.ShapeDtypeStruct((fan_y, rows, chans), BF16),
        in_specs=[VM] * 6, out_specs=HB,
        scratch_shapes=[
            pltpu.VMEM((modes, chans), F32), pltpu.VMEM((rows, chans), BF16), sem((fan_y,)),
        ],
        compiler_params=small,
        cost_estimate=cost(10_000_000, 1_000_000),
    )(ends_in, marks, residues, decay_rate, base, first)
    pay_in = lax.all_to_all(pay, "y", 0, 0)
    cuts[0] = pl.pallas_call(
        lambda *refs: own_kernel(fan_x, fan_y, *refs),
        name="own",
        out_shape=jax.ShapeDtypeStruct((2 * feats, depth), BF16),
        in_specs=[HB], out_specs=VM,
        scratch_shapes=[sem((2 * fan_y,))],
        compiler_params=small,
        cost_estimate=cost(100_000, 1_000_000),
    )(w_in)
    own = jnp.concatenate([a[:feats] for a in cuts], axis=0)
    give = jnp.concatenate([a[feats:] for a in cuts], axis=0)
    got = lax.ppermute(give, "c", [(0, 1), (1, 0)])
    keep, give = pl.pallas_call(
        lambda *refs: product_kernel(fan_x, *refs),
        name="product",
        out_shape=(
            jax.ShapeDtypeStruct((fan_x, rows, feats), F32),
            jax.ShapeDtypeStruct((fan_x, rows, feats), BF16),
        ),
        in_specs=[VM] * 3, out_specs=(VM, VM),
        scratch_shapes=[pltpu.VMEM((rows, depth), BF16)],
        compiler_params=small,
        cost_estimate=cost(4 * rows * depth * fan_x * feats, 4_000_000),
    )(pay_in, own, got)
    swapped = lax.ppermute(give, "c", [(0, 1), (1, 0)])
    taps = pl.pallas_call(
        lambda *refs: taps_kernel(rows, *refs),
        name="taps",
        out_shape=jax.ShapeDtypeStruct((modes, chans), F32),
        in_specs=[VM] * 3, out_specs=VM,
        compiler_params=small,
        cost_estimate=cost(1_000_000, 300_000),
    )(ends_in, marks, decay_rate)
    parts = pl.pallas_call(
        join_kernel,
        name="join",
        out_shape=tuple(
            jax.ShapeDtypeStruct((rows, feats), BF16 if k else F32) for k in range(fan_x)
        ),
        in_specs=[VM] * 2, out_specs=(VM,) * fan_x,
        compiler_params=small,
        cost_estimate=cost(1_000_000, 2_000_000),
    )(keep, swapped)
    parts = list(parts)
    for k in (2, 1, 3):
        parts[k] = lax.ppermute(parts[k], "x", [(i, (i - k) % fan_x) for i in range(fan_x)])
    d_input = pl.pallas_call(
        sum_kernel,
        name="total",
        out_shape=jax.ShapeDtypeStruct((rows, feats), BF16),
        in_specs=[VM] * fan_x, out_specs=VM,
        compiler_params=small,
        cost_estimate=cost(1_000_000, 900_000),
    )(*parts)
    return d_input, taps


def solution(mesh):
    grid = (16, 4, 8, 2)
    fine = Mesh(mesh.devices.reshape(grid), ("z", "x", "y", "c"))
    head = ("x", "y", "c")
    return jax.shard_map(
        device,
        mesh=fine,
        in_specs=(P("z", head), P("z", head), P(None, head), P(None, head), P(), P(head, None)),
        out_specs=(P("z", head), P(None, head)),
        check_vma=False,
    )
```
